32 devices in a mesh: arrays: 2 (over y), tm: 8 (over z, x), chan: 2 (over core).
Axes of the slice: x: 2, y: 2, z: 4, core: 2. Of those that a mesh axis runs over, the one named last changes fastest.
Arguments:
- spectra: bfloat16 [128, 256, 2, 128], P(('arrays', 'tm'), 'chan'), parts along dimension 0, may hold values from -40 to 40
- offsets: int32 [128], P(('arrays', 'tm')), parts along dimension 0, may hold values from 0 to 63
- channel_group: int32 [512], P(('arrays', 'chan')), parts along dimension 0, may hold values from 0 to 7
Outputs:
- stack: float32 [128, 48, 128], P(('arrays', 'tm', 'chan')), parts along dimension 0
The draws below stay inside these ranges and needn't reach their ends.
There are 2 independent parts, one for each index of `arrays`. The reference program is written for one: setup_inputs(seed, part) draws one part's arguments, and reference() takes and returns one part's arrays. A program takes and returns all parts, laid end to end along the dimension named above; each array names one. Nothing has to cross between parts.
All inputs are finite; a program needn't handle non-finite values.
Results may differ from the reference program's by a relative error of at most 0.0075.
Values may be sent and summed in bfloat16 or wider, within the bound.
A program may use at most 64 MiB of HBM per device.

```python
import math
import jax
import jax.numpy as jnp
from jax import lax

F = 128
LAGS = 128
GROUPS = 8
BAND = 48
WINDOWS = 64
CHANNELS = 256


def draw_spectra(key, part):
    key_amplitude = jax.random.fold_in(key, 11)
    key_values = jax.random.fold_in(key, 12)
    amplitude = jnp.exp(jax.random.uniform(key_amplitude, (WINDOWS, CHANNELS, 1, 1), jnp.float32, math.log(0.1), math.log(10.0)))
    values = jnp.clip(jax.random.normal(key_values, (WINDOWS, CHANNELS, 2, F), jnp.float32), -4.0, 4.0)
    return (amplitude * values).astype(jnp.bfloat16)


def plant(result, key, low, high):
    longest = result.shape.index(max(result.shape))
    spots = []
    for shift in (0, 1):
        where = [jax.random.randint(jax.random.fold_in(key, axis), (), 0, length) for axis, length in enumerate(result.shape)]
        where[longest] = (where[longest] + shift) % result.shape[longest]
        spots.append(tuple(where))
    return result.at[spots[0]].set(low).at[spots[1]].set(high)


def setup_inputs(seed: int = 0, part: int = 0) -> dict:
    key_of = jax.random.split(jax.random.key(seed), 4)
    part_splits = jax.random.split(jax.random.fold_in(key_of[3], part), 4)
    return {
        "spectra": draw_spectra(jax.random.fold_in(jax.random.fold_in(key_of[3], part), 71), part),
        "offsets": plant(jax.random.randint(part_splits[1], (WINDOWS,), 0, LAGS // 2), jax.random.fold_in(part_splits[1], 1), 0, (LAGS // 2) - 1).astype(jnp.int32),
        "channel_group": plant(jax.random.randint(part_splits[2], (CHANNELS,), 0, GROUPS), jax.random.fold_in(part_splits[2], 1), 0, GROUPS - 1).astype(jnp.int32),
    }


epsilon = 1e-05

def lag_table(freq_bins, lag_count):
    frequency = jnp.arange(freq_bins, dtype=jnp.int32)[:, None]
    lag_shift = jnp.arange(lag_count, dtype=jnp.int32)[None, :] - lag_count // 2
    phase_turns = jnp.mod(frequency * lag_shift, 2 * freq_bins).astype(jnp.float32)
    phase_angle = jnp.pi * phase_turns / freq_bins
    normaliser = 1.0 / math.sqrt(freq_bins)
    lag_rows = jnp.concatenate([jnp.cos(phase_angle) * normaliser, -jnp.sin(phase_angle) * normaliser], axis=0)
    return lag_rows.astype(jnp.bfloat16)

def align_spectra(spectra, offsets, scales):
    freq_bins = spectra.shape[3]
    frequency = jnp.arange(freq_bins, dtype=jnp.int32)[None, :]
    phase_turns = jnp.mod(offsets[:, None] * frequency, 2 * freq_bins).astype(jnp.float32)
    phase_angle = jnp.pi * phase_turns / freq_bins
    cosine = jnp.cos(phase_angle)[:, None, :]
    sine_part = jnp.sin(phase_angle)[:, None, :]
    real_part = spectra[:, :, 0, :].astype(jnp.float32)
    imag_part = spectra[:, :, 1, :].astype(jnp.float32)
    weight = scales[:, :, None]
    out_real = weight * (real_part * cosine + imag_part * sine_part)
    out_imag = weight * (imag_part * cosine - real_part * sine_part)
    return jnp.stack([out_real, out_imag], axis=2).astype(jnp.bfloat16)

def window_terms(current, band_rows, lag_rows):
    left_real = current[None, :, 0, :].astype(jnp.float32)
    left_imag = current[None, :, 1, :].astype(jnp.float32)
    right_real = band_rows[:, :, 0, :].astype(jnp.float32)
    right_imag = band_rows[:, :, 1, :].astype(jnp.float32)
    prod_real = left_real * right_real + left_imag * right_imag
    prod_imag = left_imag * right_real - left_real * right_imag
    cross_spec = jnp.stack([prod_real, prod_imag], axis=2).astype(jnp.bfloat16)
    flattened = cross_spec.reshape(band_rows.shape[0] * band_rows.shape[1], 2 * band_rows.shape[3])
    lagged = jnp.dot(flattened.astype(jnp.float32), lag_rows.astype(jnp.float32), precision=lax.Precision.HIGHEST)
    lagged = lagged.reshape(band_rows.shape[0], band_rows.shape[1], lag_rows.shape[1])
    return lax.optimization_barrier(jnp.sum(lagged * lagged, axis=1))

def reference(spectra, offsets, channel_group):
    chan_power = lax.optimization_barrier(jnp.sum(jnp.square(spectra.astype(jnp.float32)), axis=(2, 3)))
    onehot = (channel_group[:, None] == jnp.arange(GROUPS, dtype=jnp.int32)[None, :]).astype(jnp.float32)
    group_total = jnp.dot(chan_power, onehot, precision=lax.Precision.HIGHEST)
    energy = group_total * (GROUPS / (F * CHANNELS))
    scales = jnp.dot(lax.rsqrt(energy + epsilon), onehot.T, precision=lax.Precision.HIGHEST)
    aligned = align_spectra(spectra, offsets, scales)
    padded = jnp.concatenate([jnp.zeros((BAND, CHANNELS, 2, F), jnp.bfloat16), aligned], axis=0)
    lag_rows = lag_table(F, LAGS)

    def one_window(window):
        current = lax.dynamic_index_in_dim(aligned, window, 0, keepdims=False)
        band_rows = lax.dynamic_slice_in_dim(padded, window, BAND, 0)
        return window_terms(current, band_rows, lag_rows)
    summed = lax.map(one_window, jnp.arange(WINDOWS, dtype=jnp.int32))
    return summed * (1.0 / CHANNELS)
```

```python
import functools
import math

import jax
import jax.numpy as jnp
from jax import lax
from jax.experimental import pallas as pl
from jax.experimental.pallas import tpu as pltpu
from jax.sharding import PartitionSpec as P

LAGS = 128
GROUPS = 8
SPAN = 6


epsilon = 1e-05


def shifted(value, axis, steps):
    count = lax.axis_size(axis)
    initial, last = (max(0, -steps), min(count, count - steps))
    return lax.ppermute(value, axis, [(source, source + steps) for source in range(initial, last)])


def lag_table(freq_bins, lag_count):
    frequency = jnp.arange(freq_bins, dtype=jnp.int32)[:, None]
    lag_shift = jnp.arange(lag_count, dtype=jnp.int32)[None, :] - lag_count // 2
    phase_turns = jnp.mod(frequency * lag_shift, 2 * freq_bins).astype(jnp.float32)
    phase_angle = jnp.pi * phase_turns / freq_bins
    normaliser = 1.0 / math.sqrt(freq_bins)
    lag_rows = jnp.concatenate(
        [jnp.cos(phase_angle) * normaliser, -jnp.sin(phase_angle) * normaliser], axis=0
    )
    return lag_rows.astype(jnp.bfloat16)


def align_spectra(spectra, offsets, scales):
    freq_bins = spectra.shape[3]
    frequency = jnp.arange(freq_bins, dtype=jnp.int32)[None, :]
    phase_turns = jnp.mod(offsets[:, None] * frequency, 2 * freq_bins).astype(jnp.float32)
    phase_angle = jnp.pi * phase_turns / freq_bins
    cosine = jnp.cos(phase_angle)[:, None, :]
    sine_part = jnp.sin(phase_angle)[:, None, :]
    real_part = spectra[:, :, 0, :].astype(jnp.float32)
    imag_part = spectra[:, :, 1, :].astype(jnp.float32)
    weight = scales[:, :, None]
    out_real = weight * (real_part * cosine + imag_part * sine_part)
    out_imag = weight * (imag_part * cosine - real_part * sine_part)
    return jnp.stack([out_real, out_imag], axis=2).astype(jnp.bfloat16)


def window_terms(current, band_rows, lag_rows):
    left_real = current[None, :, 0, :].astype(jnp.float32)
    left_imag = current[None, :, 1, :].astype(jnp.float32)
    right_real = band_rows[:, :, 0, :].astype(jnp.float32)
    right_imag = band_rows[:, :, 1, :].astype(jnp.float32)
    prod_real = left_real * right_real + left_imag * right_imag
    prod_imag = left_imag * right_real - left_real * right_imag
    cross_spec = jnp.stack([prod_real, prod_imag], axis=2).astype(jnp.bfloat16)
    flattened = cross_spec.reshape(band_rows.shape[0] * band_rows.shape[1], 2 * band_rows.shape[3])
    lagged = jnp.dot(flattened, lag_rows, preferred_element_type=jnp.float32)
    lagged = lagged.reshape(band_rows.shape[0], band_rows.shape[1], lag_rows.shape[1])
    return jnp.sum(lagged * lagged, axis=1)


def ring_shards(spectra, offsets, channel_group):
    windows = spectra.shape[0]
    local_chans = spectra.shape[1]
    freq_bins = spectra.shape[3]
    chan_count = lax.axis_size("chan")
    channels = local_chans * chan_count
    onehot = (channel_group[:, None] == jnp.arange(GROUPS, dtype=jnp.int32)[None, :]).astype(
        jnp.float32
    )
    chan_power = jnp.sum(jnp.square(spectra.astype(jnp.float32)), axis=(2, 3))
    partial_value = jnp.dot(chan_power, onehot, precision=lax.Precision.HIGHEST)
    group_total = lax.psum(partial_value, "chan")
    energy = group_total * (GROUPS / (freq_bins * channels))
    scales = jnp.dot(lax.rsqrt(energy + epsilon), onehot.T, precision=lax.Precision.HIGHEST)
    aligned = align_spectra(spectra, offsets, scales)
    earlier = []
    carried = aligned
    for distance in range(SPAN):
        carried = shifted(carried, "tm", 1)
        earlier.append(carried)
    buffer = jnp.concatenate(earlier[::-1] + [aligned], axis=0)
    lag_rows = lag_table(freq_bins, LAGS)
    band_len = SPAN * windows

    def one_window(window):
        current = lax.dynamic_index_in_dim(aligned, window, 0, keepdims=False)
        band_rows = lax.dynamic_slice_in_dim(buffer, window, band_len, 0)
        return window_terms(current, band_rows, lag_rows) * (1.0 / channels)

    return lax.psum_scatter(
        lax.map(
            one_window, jnp.arange(lax.axis_size("chan") * (windows // chan_count), dtype=jnp.int32)
        ).astype(jnp.bfloat16),
        "chan",
        scatter_dimension=0,
        tiled=True,
    ).astype(jnp.float32)


HIGHEST = lax.Precision.HIGHEST


def phase_of(turns, freq_bins):
    period = 2.0 * freq_bins
    return (jnp.pi / freq_bins) * (turns - period * jnp.floor(turns / period))


def kernel(
    n, chans, windows, share, freq_bins, cores,
    x_ref, off_ref, group_ref, out_ref,
    local, wide, raw, unpacked, tile, tiles, table, aligned, part, half_out, half_in, sum_out, sum_in,
    local_sem, keep_sem, x_send, x_recv, e_send, e_recv, h_send, h_recv, s_send, s_recv,
):
    me = lax.axis_index("tm")
    core = lax.axis_index("chan")
    total = n * windows
    band = SPAN * windows
    block = 2 * windows
    blocks = band // block
    pad = block
    mine = windows // cores
    lanes = freq_bins

    load = pltpu.make_async_copy(x_ref, local, local_sem)
    load.start()
    keep = pltpu.make_async_copy(x_ref.at[:, pl.ds(me * 2 * share, 2 * share), :], raw.at[me], keep_sem)
    keep.start()

    barrier = pltpu.get_barrier_semaphore()
    for d in range(n):
        for k in range(cores):
            if d or k:
                pl.semaphore_signal(
                    barrier, inc=1,
                    device_id={"tm": lax.rem(me + d, n), "chan": lax.rem(core + k, cores)},
                    device_id_type=pl.DeviceIdType.MESH,
                )
    pl.semaphore_wait(barrier, n * cores - 1)

    def x_copy(there, slot):
        return pltpu.make_async_remote_copy(
            src_ref=x_ref.at[:, pl.ds(there * 2 * share, 2 * share), :],
            dst_ref=raw.at[slot],
            send_sem=x_send.at[there],
            recv_sem=x_recv.at[slot],
            device_id={"tm": there},
            device_id_type=pl.DeviceIdType.MESH,
        )

    for d in range(1, n):
        x_copy(lax.rem(me + d, n), me).start()

    load.wait()
    for w in range(windows):
        wide[pl.ds(w * 2 * chans, 2 * chans), :] = local[w].astype(jnp.float32)
    lane = lax.broadcasted_iota(jnp.int32, (windows, lanes), 1)
    row = lax.broadcasted_iota(jnp.int32, (windows, lanes), 0)

    def power_step(c, held):
        real = wide[pl.ds(2 * c, windows, stride=2 * chans), :]
        imag = wide[pl.ds(2 * c + 1, windows, stride=2 * chans), :]
        power = jnp.sum(real * real + imag * imag, axis=1, keepdims=True)
        return jnp.where(lane == c, power, held)

    chan_power = lax.fori_loop(0, chans, power_step, jnp.zeros((windows, lanes), jnp.float32), unroll=8)
    group_id = lax.broadcasted_iota(jnp.int32, (lanes, chans), 0)
    onehot = (group_id == group_ref[...]).astype(jnp.float32)
    totals = lax.dot_general(
        chan_power, onehot, (((1,), (1,)), ((), ())), precision=HIGHEST, preferred_element_type=jnp.float32
    )
    for w in range(windows):
        totals = jnp.where((lane == lanes - 1) & (row == w), off_ref[w].astype(jnp.float32), totals)
    tile[...] = totals

    def e_copy(there, other, slot):
        return pltpu.make_async_remote_copy(
            src_ref=tile,
            dst_ref=tiles.at[slot],
            send_sem=e_send.at[there * cores + other],
            recv_sem=e_recv.at[slot],
            device_id={"tm": there, "chan": other},
            device_id_type=pl.DeviceIdType.MESH,
        )

    def others():
        for d in range(n):
            for k in range(cores):
                if d or k:
                    yield lax.rem(me + d, n), lax.rem(core + k, cores)

    for there, other in others():
        e_copy(there, other, me * cores + core).start()
    tiles[me * cores + core] = totals

    frequency = lax.broadcasted_iota(jnp.int32, (freq_bins, LAGS), 0)
    shift = lax.broadcasted_iota(jnp.int32, (freq_bins, LAGS), 1) - LAGS // 2
    angle = phase_of((frequency * shift).astype(jnp.float32), freq_bins)
    normaliser = 1.0 / math.sqrt(freq_bins)
    table[pl.ds(0, freq_bins), :] = (jnp.cos(angle) * normaliser).astype(jnp.bfloat16)
    table[pl.ds(freq_bins, freq_bins), :] = (-jnp.sin(angle) * normaliser).astype(jnp.bfloat16)
    aligned[:, :, pl.ds(0, pad), :] = jnp.zeros((share, 2, pad, freq_bins), jnp.float32)
    part[...] = jnp.zeros_like(part)

    my_onehot = (group_id == pltpu.roll(group_ref[...], lax.rem(chans - me * share, chans), 1)).astype(jnp.float32)
    bins = lax.broadcasted_iota(jnp.int32, (windows, freq_bins), 1).astype(jnp.float32)
    keep.wait()
    for there, other in others():
        e_copy(there, other, there * cores + other).wait_recv()

    def align_step(i, carry):
        t = lax.rem(me + n - i, n)

        @pl.when(i > 0)
        def _():
            x_copy(t, t).wait_recv()

        for w in range(windows):
            unpacked[pl.ds(w * 2 * share, 2 * share), :] = raw[t, w].astype(jnp.float32)
        first = tiles[t * cores]
        summed = first
        for k in range(1, cores):
            summed = summed + tiles[t * cores + k]
        energy = summed * (GROUPS / (freq_bins * chans * cores))
        scales = jnp.dot(
            lax.rsqrt(energy + epsilon), my_onehot, precision=HIGHEST, preferred_element_type=jnp.float32
        )
        theta = phase_of(bins * first[:, lanes - 1 : lanes], freq_bins)
        cosine = jnp.cos(theta)
        sine = jnp.sin(theta)
        for c in range(share):
            real = unpacked[pl.ds(2 * c, windows, stride=2 * share), :]
            imag = unpacked[pl.ds(2 * c + 1, windows, stride=2 * share), :]
            weight = scales[:, c : c + 1]
            out_real = weight * (real * cosine + imag * sine)
            out_imag = weight * (imag * cosine - real * sine)
            place = pl.ds(pl.multiple_of(pad + t * windows, windows), windows)
            aligned[c, 0, place, :] = out_real.astype(jnp.bfloat16).astype(jnp.float32)
            aligned[c, 1, place, :] = out_imag.astype(jnp.bfloat16).astype(jnp.float32)
        return carry

    lax.fori_loop(0, n, align_step, 0)

    def pair_block(w, k):
        start = pad + w - band + k * block
        rows = []
        for c in range(share):
            left_real = aligned[c, 0, pl.ds(pad + w, 1), :]
            left_imag = aligned[c, 1, pl.ds(pad + w, 1), :]
            right_real = aligned[c, 0, pl.ds(start, block), :]
            right_imag = aligned[c, 1, pl.ds(start, block), :]
            prod_real = left_real * right_real + left_imag * right_imag
            prod_imag = left_imag * right_real - left_real * right_imag
            rows.append(
                jnp.concatenate([prod_real.astype(jnp.bfloat16), prod_imag.astype(jnp.bfloat16)], axis=1)
            )
        lagged = jnp.dot(jnp.concatenate(rows, axis=0), table[...], preferred_element_type=jnp.float32)
        lagged = lagged.reshape(share, block, LAGS)
        part[w, pl.ds(pl.multiple_of(k * block, block), block), :] = jnp.sum(lagged * lagged, axis=0)

    def h_copy(t):
        return pltpu.make_async_remote_copy(
            src_ref=half_out.at[t],
            dst_ref=half_in.at[t],
            send_sem=h_send.at[t],
            recv_sem=h_recv.at[t],
            device_id={"chan": 1 - core},
            device_id_type=pl.DeviceIdType.MESH,
        )

    def s_copy(t, slot):
        return pltpu.make_async_remote_copy(
            src_ref=sum_out.at[t],
            dst_ref=sum_in.at[slot],
            send_sem=s_send.at[t],
            recv_sem=s_recv.at[slot],
            device_id={"tm": t},
            device_id_type=pl.DeviceIdType.MESH,
        )

    def pass_on(t):
        h_copy(t).wait_recv()
        return part[pl.ds(t * windows + core * mine, mine)] + half_in[t].astype(jnp.float32)

    def stage(i, carry):
        t = lax.rem(me + 1 + i, n)

        def one_window(j, held):
            w = t * windows + j
            first = jnp.maximum(band - w, 0) // block

            def one_block(k, inner):
                pair_block(w, k)
                return inner

            lax.fori_loop(first, blocks, one_block, 0)
            return held

        lax.fori_loop(0, windows, one_window, 0)
        half_out[t] = part[pl.ds(t * windows + (1 - core) * mine, mine)].astype(jnp.bfloat16)
        h_copy(t).start()

        @pl.when(i > 0)
        def _():
            before = lax.rem(me + i, n)
            sum_out[before] = pass_on(before).astype(jnp.bfloat16)
            s_copy(before, me).start()

        return carry

    lax.fori_loop(0, n, stage, 0)
    result = pass_on(me)
    for d in range(1, n):
        s = lax.rem(me + n - d, n)
        s_copy(s, s).wait_recv()
        result = result + sum_in[s].astype(jnp.float32)
    out_ref[...] = result * (1.0 / (chans * cores))

    for d in range(1, n):
        t = lax.rem(me + d, n)
        x_copy(t, me).wait_send()
        s_copy(t, me).wait_send()
    for t in range(n):
        h_copy(t).wait_send()
    for there, other in others():
        e_copy(there, other, me * cores + core).wait_send()


def spread_shards(spectra, offsets, channel_group):
    windows, chans, _, freq_bins = spectra.shape
    n = lax.axis_size("tm")
    cores = lax.axis_size("chan")
    share = chans // n
    total = n * windows
    band = SPAN * windows
    mine = windows // cores
    dma = pltpu.SemaphoreType.DMA
    return pl.pallas_call(
        functools.partial(kernel, n, chans, windows, share, freq_bins, cores),
        out_shape=jax.ShapeDtypeStruct((mine, band, LAGS), jnp.float32),
        in_specs=[
            pl.BlockSpec(memory_space=pl.ANY),
            pl.BlockSpec(memory_space=pltpu.SMEM),
            pl.BlockSpec(memory_space=pltpu.VMEM),
        ],
        out_specs=pl.BlockSpec(memory_space=pltpu.VMEM),
        scratch_shapes=[
            pltpu.VMEM((windows, 2 * chans, freq_bins), jnp.bfloat16),
            pltpu.VMEM((windows * 2 * chans, freq_bins), jnp.float32),
            pltpu.VMEM((n, windows, 2 * share, freq_bins), jnp.bfloat16),
            pltpu.VMEM((windows * 2 * share, freq_bins), jnp.float32),
            pltpu.VMEM((windows, freq_bins), jnp.float32),
            pltpu.VMEM((n * cores, windows, freq_bins), jnp.float32),
            pltpu.VMEM((2 * freq_bins, LAGS), jnp.bfloat16),
            pltpu.VMEM((share, 2, total + 2 * windows, freq_bins), jnp.float32),
            pltpu.VMEM((total, band, LAGS), jnp.float32),
            pltpu.VMEM((n, mine, band, LAGS), jnp.bfloat16),
            pltpu.VMEM((n, mine, band, LAGS), jnp.bfloat16),
            pltpu.VMEM((n, mine, band, LAGS), jnp.bfloat16),
            pltpu.VMEM((n, mine, band, LAGS), jnp.bfloat16),
            dma, dma, dma((n,)), dma((n,)), dma((n * cores,)), dma((n * cores,)),
            dma((n,)), dma((n,)), dma((n,)), dma((n,)),
        ],
        compiler_params=pltpu.CompilerParams(
            collective_id=0, has_side_effects=True, vmem_limit_bytes=56 * 1024 * 1024
        ),
    )(spectra.reshape(windows, 2 * chans, freq_bins), offsets, channel_group.reshape(1, chans))


def shards(spectra, offsets, channel_group):
    windows, chans, _, freq_bins = spectra.shape
    n = lax.axis_size("tm")
    fits = (
        chans == freq_bins == LAGS == 128
        and windows == 8
        and lax.axis_size("chan") == 2
        and chans % n == 0
        and chans // n >= 8
    )
    return (spread_shards if fits else ring_shards)(spectra, offsets, channel_group)


def solution(mesh):
    placed = (P(("arrays", "tm"), "chan", None, None), P(("arrays", "tm")), P(("arrays", "chan")))
    return jax.shard_map(
        shards,
        mesh=mesh,
        in_specs=placed,
        out_specs=P(("arrays", "tm", "chan"), None, None),
        check_vma=False,
    )
```

```python
import functools
import math

import jax
import jax.numpy as jnp
from jax import lax
from jax.experimental import pallas as pl
from jax.experimental.pallas import tpu as pltpu
from jax.sharding import PartitionSpec as P

LAGS = 128
GROUPS = 8
SPAN = 6


epsilon = 1e-05


def shifted(value, axis, steps):
    count = lax.axis_size(axis)
    initial, last = (max(0, -steps), min(count, count - steps))
    return lax.ppermute(value, axis, [(source, source + steps) for source in range(initial, last)])


def lag_table(freq_bins, lag_count):
    frequency = jnp.arange(freq_bins, dtype=jnp.int32)[:, None]
    lag_shift = jnp.arange(lag_count, dtype=jnp.int32)[None, :] - lag_count // 2
    phase_turns = jnp.mod(frequency * lag_shift, 2 * freq_bins).astype(jnp.float32)
    phase_angle = jnp.pi * phase_turns / freq_bins
    normaliser = 1.0 / math.sqrt(freq_bins)
    lag_rows = jnp.concatenate(
        [jnp.cos(phase_angle) * normaliser, -jnp.sin(phase_angle) * normaliser], axis=0
    )
    return lag_rows.astype(jnp.bfloat16)


def align_spectra(spectra, offsets, scales):
    freq_bins = spectra.shape[3]
    frequency = jnp.arange(freq_bins, dtype=jnp.int32)[None, :]
    phase_turns = jnp.mod(offsets[:, None] * frequency, 2 * freq_bins).astype(jnp.float32)
    phase_angle = jnp.pi * phase_turns / freq_bins
    cosine = jnp.cos(phase_angle)[:, None, :]
    sine_part = jnp.sin(phase_angle)[:, None, :]
    real_part = spectra[:, :, 0, :].astype(jnp.float32)
    imag_part = spectra[:, :, 1, :].astype(jnp.float32)
    weight = scales[:, :, None]
    out_real = weight * (real_part * cosine + imag_part * sine_part)
    out_imag = weight * (imag_part * cosine - real_part * sine_part)
    return jnp.stack([out_real, out_imag], axis=2).astype(jnp.bfloat16)


def window_terms(current, band_rows, lag_rows):
    left_real = current[None, :, 0, :].astype(jnp.float32)
    left_imag = current[None, :, 1, :].astype(jnp.float32)
    right_real = band_rows[:, :, 0, :].astype(jnp.float32)
    right_imag = band_rows[:, :, 1, :].astype(jnp.float32)
    prod_real = left_real * right_real + left_imag * right_imag
    prod_imag = left_imag * right_real - left_real * right_imag
    cross_spec = jnp.stack([prod_real, prod_imag], axis=2).astype(jnp.bfloat16)
    flattened = cross_spec.reshape(band_rows.shape[0] * band_rows.shape[1], 2 * band_rows.shape[3])
    lagged = jnp.dot(flattened, lag_rows, preferred_element_type=jnp.float32)
    lagged = lagged.reshape(band_rows.shape[0], band_rows.shape[1], lag_rows.shape[1])
    return jnp.sum(lagged * lagged, axis=1)


def ring_shards(spectra, offsets, channel_group):
    windows = spectra.shape[0]
    local_chans = spectra.shape[1]
    freq_bins = spectra.shape[3]
    chan_count = lax.axis_size("chan")
    channels = local_chans * chan_count
    onehot = (channel_group[:, None] == jnp.arange(GROUPS, dtype=jnp.int32)[None, :]).astype(
        jnp.float32
    )
    chan_power = jnp.sum(jnp.square(spectra.astype(jnp.float32)), axis=(2, 3))
    partial_value = jnp.dot(chan_power, onehot, precision=lax.Precision.HIGHEST)
    group_total = lax.psum(partial_value, "chan")
    energy = group_total * (GROUPS / (freq_bins * channels))
    scales = jnp.dot(lax.rsqrt(energy + epsilon), onehot.T, precision=lax.Precision.HIGHEST)
    aligned = align_spectra(spectra, offsets, scales)
    earlier = []
    carried = aligned
    for distance in range(SPAN):
        carried = shifted(carried, "tm", 1)
        earlier.append(carried)
    buffer = jnp.concatenate(earlier[::-1] + [aligned], axis=0)
    lag_rows = lag_table(freq_bins, LAGS)
    band_len = SPAN * windows

    def one_window(window):
        current = lax.dynamic_index_in_dim(aligned, window, 0, keepdims=False)
        band_rows = lax.dynamic_slice_in_dim(buffer, window, band_len, 0)
        return window_terms(current, band_rows, lag_rows) * (1.0 / channels)

    return lax.psum_scatter(
        lax.map(
            one_window, jnp.arange(lax.axis_size("chan") * (windows // chan_count), dtype=jnp.int32)
        ).astype(jnp.bfloat16),
        "chan",
        scatter_dimension=0,
        tiled=True,
    ).astype(jnp.float32)


HIGHEST = lax.Precision.HIGHEST


def phase_of(turns, freq_bins):
    period = 2.0 * freq_bins
    return (jnp.pi / freq_bins) * (turns - period * jnp.floor(turns / period))


def kernel(
    n, chans, windows, share, freq_bins, cores,
    x_ref, off_ref, group_ref, out_ref,
    local, wide, raw, unpacked, tile, tiles, table, right, left, part, half_out, half_in, sum_out, sum_in,
    local_sem, keep_sem, x_send, x_recv, e_send, e_recv, h_send, h_recv, s_send, s_recv,
):
    me = lax.axis_index("tm")
    core = lax.axis_index("chan")
    band = SPAN * windows
    mine = windows // cores
    lanes = freq_bins

    load = pltpu.make_async_copy(x_ref, local, local_sem)
    load.start()
    keep = pltpu.make_async_copy(x_ref.at[:, pl.ds(me * 2 * share, 2 * share), :], raw.at[me], keep_sem)
    keep.start()

    barrier = pltpu.get_barrier_semaphore()
    for d in range(n):
        for k in range(cores):
            if d or k:
                pl.semaphore_signal(
                    barrier, inc=1,
                    device_id={"tm": lax.rem(me + d, n), "chan": lax.rem(core + k, cores)},
                    device_id_type=pl.DeviceIdType.MESH,
                )
    pl.semaphore_wait(barrier, n * cores - 1)

    def x_copy(there, slot):
        return pltpu.make_async_remote_copy(
            src_ref=x_ref.at[:, pl.ds(there * 2 * share, 2 * share), :],
            dst_ref=raw.at[slot],
            send_sem=x_send.at[there],
            recv_sem=x_recv.at[slot],
            device_id={"tm": there},
            device_id_type=pl.DeviceIdType.MESH,
        )

    for d in range(1, n):
        x_copy(lax.rem(me + d, n), me).start()

    load.wait()
    for w in range(windows):
        wide[pl.ds(w * 2 * chans, 2 * chans), :] = local[w].astype(jnp.float32)
    lane = lax.broadcasted_iota(jnp.int32, (windows, lanes), 1)
    row = lax.broadcasted_iota(jnp.int32, (windows, lanes), 0)

    def power_step(c, held):
        real = wide[pl.ds(2 * c, windows, stride=2 * chans), :]
        imag = wide[pl.ds(2 * c + 1, windows, stride=2 * chans), :]
        power = jnp.sum(real * real + imag * imag, axis=1, keepdims=True)
        return jnp.where(lane == c, power, held)

    chan_power = lax.fori_loop(0, chans, power_step, jnp.zeros((windows, lanes), jnp.float32), unroll=8)
    group_id = lax.broadcasted_iota(jnp.int32, (lanes, chans), 0)
    onehot = (group_id == group_ref[...]).astype(jnp.float32)
    totals = lax.dot_general(
        chan_power, onehot, (((1,), (1,)), ((), ())), precision=HIGHEST, preferred_element_type=jnp.float32
    )
    for w in range(windows):
        totals = jnp.where((lane == lanes - 1) & (row == w), off_ref[w].astype(jnp.float32), totals)
    tile[...] = totals

    def e_copy(there, other, slot):
        return pltpu.make_async_remote_copy(
            src_ref=tile,
            dst_ref=tiles.at[slot],
            send_sem=e_send.at[there * cores + other],
            recv_sem=e_recv.at[slot],
            device_id={"tm": there, "chan": other},
            device_id_type=pl.DeviceIdType.MESH,
        )

    def others():
        for d in range(n):
            for k in range(cores):
                if d or k:
                    yield lax.rem(me + d, n), lax.rem(core + k, cores)

    for there, other in others():
        e_copy(there, other, me * cores + core).start()
    tiles[me * cores + core] = totals

    frequency = lax.broadcasted_iota(jnp.int32, (freq_bins, LAGS), 0)
    shift = lax.broadcasted_iota(jnp.int32, (freq_bins, LAGS), 1) - LAGS // 2
    angle = phase_of((frequency * shift).astype(jnp.float32), freq_bins)
    normaliser = 1.0 / math.sqrt(freq_bins)
    table[pl.ds(0, freq_bins), :] = (jnp.cos(angle) * normaliser).astype(jnp.bfloat16)
    table[pl.ds(freq_bins, freq_bins), :] = (-jnp.sin(angle) * normaliser).astype(jnp.bfloat16)
    part[...] = jnp.zeros_like(part)

    my_onehot = (group_id == pltpu.roll(group_ref[...], lax.rem(chans - me * share, chans), 1)).astype(jnp.float32)
    bins = lax.broadcasted_iota(jnp.int32, (windows, freq_bins), 1).astype(jnp.float32)
    keep.wait()
    for there, other in others():
        e_copy(there, other, there * cores + other).wait_recv()

    def align_step(i, carry):
        t = lax.rem(me + n - i, n)

        @pl.when(i > 0)
        def _():
            x_copy(t, t).wait_recv()

        for w in range(windows):
            unpacked[pl.ds(w * 2 * share, 2 * share), :] = raw[t, w].astype(jnp.float32)
        first = tiles[t * cores]
        summed = first
        for k in range(1, cores):
            summed = summed + tiles[t * cores + k]
        energy = summed * (GROUPS / (freq_bins * chans * cores))
        scales = jnp.dot(
            lax.rsqrt(energy + epsilon), my_onehot, precision=HIGHEST, preferred_element_type=jnp.float32
        )
        theta = phase_of(bins * first[:, lanes - 1 : lanes], freq_bins)
        cosine = jnp.cos(theta)
        sine = jnp.sin(theta)
        for p in range(share // 2):
            pair = []
            for c in (2 * p, 2 * p + 1):
                real = unpacked[pl.ds(2 * c, windows, stride=2 * share), :]
                imag = unpacked[pl.ds(2 * c + 1, windows, stride=2 * share), :]
                weight = scales[:, c : c + 1]
                pair.append((weight * (real * cosine + imag * sine), weight * (imag * cosine - real * sine)))
            for r in range(2):
                right[p, r, t] = jnp.concatenate([pair[0][r], pair[1][r]], axis=0).astype(jnp.bfloat16)
                for j in range(windows):
                    spread = [jnp.broadcast_to(x[r][j : j + 1, :], (windows, freq_bins)) for x in pair]
                    left[t * windows + j, p, r] = jnp.concatenate(spread, axis=0).astype(jnp.bfloat16)
        return carry

    lax.fori_loop(0, n, align_step, 0)

    def pair_block(t, s):
        rights = [(right[p, 0, s], right[p, 1, s]) for p in range(share // 2)]
        for j in range(windows):
            w = t * windows + j
            rows = []
            for p, (right_real, right_imag) in enumerate(rights):
                left_real = left[w, p, 0]
                left_imag = left[w, p, 1]
                prod_real = left_real * right_real + left_imag * right_imag
                prod_imag = left_imag * right_real - left_real * right_imag
                rows.append(jnp.concatenate([prod_real, prod_imag], axis=1))
            lagged = jnp.dot(jnp.concatenate(rows, axis=0), table[...], preferred_element_type=jnp.float32)
            lagged = lagged.reshape(share, windows, LAGS)
            place = band + windows + s * windows - w
            part[w, pl.ds(place, windows), :] = jnp.sum(lagged * lagged, axis=0)

    def h_copy(t):
        return pltpu.make_async_remote_copy(
            src_ref=half_out.at[t],
            dst_ref=half_in.at[t],
            send_sem=h_send.at[t],
            recv_sem=h_recv.at[t],
            device_id={"chan": 1 - core},
            device_id_type=pl.DeviceIdType.MESH,
        )

    def s_copy(t, slot):
        return pltpu.make_async_remote_copy(
            src_ref=sum_out.at[t],
            dst_ref=sum_in.at[slot],
            send_sem=s_send.at[t],
            recv_sem=s_recv.at[slot],
            device_id={"tm": t},
            device_id_type=pl.DeviceIdType.MESH,
        )

    def pass_on(t):
        h_copy(t).wait_recv()
        return part[pl.ds(t * windows + core * mine, mine), pl.ds(windows, band), :] + half_in[t].astype(jnp.float32)

    def stage(i, carry):
        t = lax.rem(me + 1 + i, n)

        def one_block(s, held):
            pair_block(t, s)
            return held

        lax.fori_loop(jnp.maximum(t - SPAN, 0), t + 1, one_block, 0)
        half_out[t] = part[pl.ds(t * windows + (1 - core) * mine, mine), pl.ds(windows, band), :].astype(jnp.bfloat16)
        h_copy(t).start()

        @pl.when(i > 0)
        def _():
            before = lax.rem(me + i, n)
            sum_out[before] = pass_on(before).astype(jnp.bfloat16)
            s_copy(before, me).start()

        return carry

    lax.fori_loop(0, n, stage, 0)
    result = pass_on(me)
    for d in range(1, n):
        s = lax.rem(me + n - d, n)
        s_copy(s, s).wait_recv()
        result = result + sum_in[s].astype(jnp.float32)
    out_ref[...] = result * (1.0 / (chans * cores))

    for d in range(1, n):
        t = lax.rem(me + d, n)
        x_copy(t, me).wait_send()
        s_copy(t, me).wait_send()
    for t in range(n):
        h_copy(t).wait_send()
    for there, other in others():
        e_copy(there, other, me * cores + core).wait_send()


def spread_shards(spectra, offsets, channel_group):
    windows, chans, _, freq_bins = spectra.shape
    n = lax.axis_size("tm")
    cores = lax.axis_size("chan")
    share = chans // n
    total = n * windows
    band = SPAN * windows
    mine = windows // cores
    dma = pltpu.SemaphoreType.DMA
    return pl.pallas_call(
        functools.partial(kernel, n, chans, windows, share, freq_bins, cores),
        out_shape=jax.ShapeDtypeStruct((mine, band, LAGS), jnp.float32),
        in_specs=[
            pl.BlockSpec(memory_space=pl.ANY),
            pl.BlockSpec(memory_space=pltpu.SMEM),
            pl.BlockSpec(memory_space=pltpu.VMEM),
        ],
        out_specs=pl.BlockSpec(memory_space=pltpu.VMEM),
        scratch_shapes=[
            pltpu.VMEM((windows, 2 * chans, freq_bins), jnp.bfloat16),
            pltpu.VMEM((windows * 2 * chans, freq_bins), jnp.float32),
            pltpu.VMEM((n, windows, 2 * share, freq_bins), jnp.bfloat16),
            pltpu.VMEM((windows * 2 * share, freq_bins), jnp.float32),
            pltpu.VMEM((windows, freq_bins), jnp.float32),
            pltpu.VMEM((n * cores, windows, freq_bins), jnp.float32),
            pltpu.VMEM((2 * freq_bins, LAGS), jnp.bfloat16),
            pltpu.VMEM((share // 2, 2, n, 2 * windows, freq_bins), jnp.bfloat16),
            pltpu.VMEM((total, share // 2, 2, 2 * windows, freq_bins), jnp.bfloat16),
            pltpu.VMEM((total, band + 2 * windows, LAGS), jnp.float32),
            pltpu.VMEM((n, mine, band, LAGS), jnp.bfloat16),
            pltpu.VMEM((n, mine, band, LAGS), jnp.bfloat16),
            pltpu.VMEM((n, mine, band, LAGS), jnp.bfloat16),
            pltpu.VMEM((n, mine, band, LAGS), jnp.bfloat16),
            dma, dma, dma((n,)), dma((n,)), dma((n * cores,)), dma((n * cores,)),
            dma((n,)), dma((n,)), dma((n,)), dma((n,)),
        ],
        compiler_params=pltpu.CompilerParams(
            collective_id=0, has_side_effects=True, vmem_limit_bytes=56 * 1024 * 1024
        ),
    )(spectra.reshape(windows, 2 * chans, freq_bins), offsets, channel_group.reshape(1, chans))


def shards(spectra, offsets, channel_group):
    windows, chans, _, freq_bins = spectra.shape
    n = lax.axis_size("tm")
    fits = (
        chans == freq_bins == LAGS == 128
        and windows == 8
        and lax.axis_size("chan") == 2
        and chans % n == 0
        and chans // n >= 8
    )
    return (spread_shards if fits else ring_shards)(spectra, offsets, channel_group)


def solution(mesh):
    placed = (P(("arrays", "tm"), "chan", None, None), P(("arrays", "tm")), P(("arrays", "chan")))
    return jax.shard_map(
        shards,
        mesh=mesh,
        in_specs=placed,
        out_specs=P(("arrays", "tm", "chan"), None, None),
        check_vma=False,
    )
```

```python
import functools
import math

import jax
import jax.numpy as jnp
from jax import lax
from jax.experimental import pallas as pl
from jax.experimental.pallas import tpu as pltpu
from jax.sharding import PartitionSpec as P

LAGS = 128
GROUPS = 8
SPAN = 6


epsilon = 1e-05


def shifted(value, axis, steps):
    count = lax.axis_size(axis)
    initial, last = (max(0, -steps), min(count, count - steps))
    return lax.ppermute(value, axis, [(source, source + steps) for source in range(initial, last)])


def lag_table(freq_bins, lag_count):
    frequency = jnp.arange(freq_bins, dtype=jnp.int32)[:, None]
    lag_shift = jnp.arange(lag_count, dtype=jnp.int32)[None, :] - lag_count // 2
    phase_turns = jnp.mod(frequency * lag_shift, 2 * freq_bins).astype(jnp.float32)
    phase_angle = jnp.pi * phase_turns / freq_bins
    normaliser = 1.0 / math.sqrt(freq_bins)
    lag_rows = jnp.concatenate(
        [jnp.cos(phase_angle) * normaliser, -jnp.sin(phase_angle) * normaliser], axis=0
    )
    return lag_rows.astype(jnp.bfloat16)


def align_spectra(spectra, offsets, scales):
    freq_bins = spectra.shape[3]
    frequency = jnp.arange(freq_bins, dtype=jnp.int32)[None, :]
    phase_turns = jnp.mod(offsets[:, None] * frequency, 2 * freq_bins).astype(jnp.float32)
    phase_angle = jnp.pi * phase_turns / freq_bins
    cosine = jnp.cos(phase_angle)[:, None, :]
    sine_part = jnp.sin(phase_angle)[:, None, :]
    real_part = spectra[:, :, 0, :].astype(jnp.float32)
    imag_part = spectra[:, :, 1, :].astype(jnp.float32)
    weight = scales[:, :, None]
    out_real = weight * (real_part * cosine + imag_part * sine_part)
    out_imag = weight * (imag_part * cosine - real_part * sine_part)
    return jnp.stack([out_real, out_imag], axis=2).astype(jnp.bfloat16)


def window_terms(current, band_rows, lag_rows):
    left_real = current[None, :, 0, :].astype(jnp.float32)
    left_imag = current[None, :, 1, :].astype(jnp.float32)
    right_real = band_rows[:, :, 0, :].astype(jnp.float32)
    right_imag = band_rows[:, :, 1, :].astype(jnp.float32)
    prod_real = left_real * right_real + left_imag * right_imag
    prod_imag = left_imag * right_real - left_real * right_imag
    cross_spec = jnp.stack([prod_real, prod_imag], axis=2).astype(jnp.bfloat16)
    flattened = cross_spec.reshape(band_rows.shape[0] * band_rows.shape[1], 2 * band_rows.shape[3])
    lagged = jnp.dot(flattened, lag_rows, preferred_element_type=jnp.float32)
    lagged = lagged.reshape(band_rows.shape[0], band_rows.shape[1], lag_rows.shape[1])
    return jnp.sum(lagged * lagged, axis=1)


def ring_shards(spectra, offsets, channel_group):
    windows = spectra.shape[0]
    local_chans = spectra.shape[1]
    freq_bins = spectra.shape[3]
    chan_count = lax.axis_size("chan")
    channels = local_chans * chan_count
    onehot = (channel_group[:, None] == jnp.arange(GROUPS, dtype=jnp.int32)[None, :]).astype(
        jnp.float32
    )
    chan_power = jnp.sum(jnp.square(spectra.astype(jnp.float32)), axis=(2, 3))
    partial_value = jnp.dot(chan_power, onehot, precision=lax.Precision.HIGHEST)
    group_total = lax.psum(partial_value, "chan")
    energy = group_total * (GROUPS / (freq_bins * channels))
    scales = jnp.dot(lax.rsqrt(energy + epsilon), onehot.T, precision=lax.Precision.HIGHEST)
    aligned = align_spectra(spectra, offsets, scales)
    earlier = []
    carried = aligned
    for distance in range(SPAN):
        carried = shifted(carried, "tm", 1)
        earlier.append(carried)
    buffer = jnp.concatenate(earlier[::-1] + [aligned], axis=0)
    lag_rows = lag_table(freq_bins, LAGS)
    band_len = SPAN * windows

    def one_window(window):
        current = lax.dynamic_index_in_dim(aligned, window, 0, keepdims=False)
        band_rows = lax.dynamic_slice_in_dim(buffer, window, band_len, 0)
        return window_terms(current, band_rows, lag_rows) * (1.0 / channels)

    return lax.psum_scatter(
        lax.map(
            one_window, jnp.arange(lax.axis_size("chan") * (windows // chan_count), dtype=jnp.int32)
        ).astype(jnp.bfloat16),
        "chan",
        scatter_dimension=0,
        tiled=True,
    ).astype(jnp.float32)


HIGHEST = lax.Precision.HIGHEST


def phase_of(turns, freq_bins):
    period = 2.0 * freq_bins
    return (jnp.pi / freq_bins) * (turns - period * jnp.floor(turns / period))


def kernel(
    n, chans, windows, share, freq_bins, cores,
    x_ref, off_ref, group_ref, out_ref,
    local, wide, raw, unpacked, tile, tiles, table, right, left, part, half_out, half_in, sum_out, sum_in,
    local_sem, keep_sem, x_send, x_recv, e_send, e_recv, h_send, h_recv, s_send, s_recv,
):
    me = lax.axis_index("tm")
    core = lax.axis_index("chan")
    band = SPAN * windows
    mine = windows // cores
    lanes = freq_bins

    load = pltpu.make_async_copy(x_ref, local, local_sem)
    load.start()
    keep = pltpu.make_async_copy(x_ref.at[:, pl.ds(me * 2 * share, 2 * share), :], raw.at[me], keep_sem)
    keep.start()

    barrier = pltpu.get_barrier_semaphore()
    for d in range(n):
        for k in range(cores):
            if d or k:
                pl.semaphore_signal(
                    barrier, inc=1,
                    device_id={"tm": lax.rem(me + d, n), "chan": lax.rem(core + k, cores)},
                    device_id_type=pl.DeviceIdType.MESH,
                )
    def x_copy(there, slot):
        return pltpu.make_async_remote_copy(
            src_ref=x_ref.at[:, pl.ds(there * 2 * share, 2 * share), :],
            dst_ref=raw.at[slot],
            send_sem=x_send.at[there],
            recv_sem=x_recv.at[slot],
            device_id={"tm": there},
            device_id_type=pl.DeviceIdType.MESH,
        )

    load.wait()
    for w in range(windows):
        wide[pl.ds(w * 2 * chans, 2 * chans), :] = local[w].astype(jnp.float32)
    lane = lax.broadcasted_iota(jnp.int32, (windows, lanes), 1)
    row = lax.broadcasted_iota(jnp.int32, (windows, lanes), 0)

    def power_step(c, held):
        real = wide[pl.ds(2 * c, windows, stride=2 * chans), :]
        imag = wide[pl.ds(2 * c + 1, windows, stride=2 * chans), :]
        power = jnp.sum(real * real + imag * imag, axis=1, keepdims=True)
        return jnp.where(lane == c, power, held)

    chan_power = lax.fori_loop(0, chans, power_step, jnp.zeros((windows, lanes), jnp.float32), unroll=8)
    group_id = lax.broadcasted_iota(jnp.int32, (lanes, chans), 0)
    onehot = (group_id == group_ref[...]).astype(jnp.float32)
    totals = lax.dot_general(
        chan_power, onehot, (((1,), (1,)), ((), ())), precision=HIGHEST, preferred_element_type=jnp.float32
    )
    for w in range(windows):
        totals = jnp.where((lane == lanes - 1) & (row == w), off_ref[w].astype(jnp.float32), totals)
    tile[...] = totals

    def e_copy(there, other, slot):
        return pltpu.make_async_remote_copy(
            src_ref=tile,
            dst_ref=tiles.at[slot],
            send_sem=e_send.at[there * cores + other],
            recv_sem=e_recv.at[slot],
            device_id={"tm": there, "chan": other},
            device_id_type=pl.DeviceIdType.MESH,
        )

    def others():
        for d in range(n):
            for k in range(cores):
                if d or k:
                    yield lax.rem(me + d, n), lax.rem(core + k, cores)

    pl.semaphore_wait(barrier, n * cores - 1)
    for there, other in others():
        e_copy(there, other, me * cores + core).start()
    for d in range(1, n):
        x_copy(lax.rem(me + d, n), me).start()
    tiles[me * cores + core] = totals

    frequency = lax.broadcasted_iota(jnp.int32, (freq_bins, LAGS), 0)
    shift = lax.broadcasted_iota(jnp.int32, (freq_bins, LAGS), 1) - LAGS // 2
    angle = phase_of((frequency * shift).astype(jnp.float32), freq_bins)
    normaliser = 1.0 / math.sqrt(freq_bins)
    table[pl.ds(0, freq_bins), :] = (jnp.cos(angle) * normaliser).astype(jnp.bfloat16)
    table[pl.ds(freq_bins, freq_bins), :] = (-jnp.sin(angle) * normaliser).astype(jnp.bfloat16)
    part[...] = jnp.zeros_like(part)

    my_onehot = (group_id == pltpu.roll(group_ref[...], lax.rem(chans - me * share, chans), 1)).astype(jnp.float32)
    bins = lax.broadcasted_iota(jnp.int32, (windows, freq_bins), 1).astype(jnp.float32)
    keep.wait()
    for there, other in others():
        e_copy(there, other, there * cores + other).wait_recv()

    def align_step(i, carry):
        t = lax.rem(me + n - i, n)

        @pl.when(i > 0)
        def _():
            x_copy(t, t).wait_recv()

        for w in range(windows):
            unpacked[pl.ds(w * 2 * share, 2 * share), :] = raw[t, w].astype(jnp.float32)
        first = tiles[t * cores]
        summed = first
        for k in range(1, cores):
            summed = summed + tiles[t * cores + k]
        energy = summed * (GROUPS / (freq_bins * chans * cores))
        scales = jnp.dot(
            lax.rsqrt(energy + epsilon), my_onehot, precision=HIGHEST, preferred_element_type=jnp.float32
        )
        theta = phase_of(bins * first[:, lanes - 1 : lanes], freq_bins)
        cosine = jnp.cos(theta)
        sine = jnp.sin(theta)
        for c in range(share):
            real = unpacked[pl.ds(2 * c, windows, stride=2 * share), :]
            imag = unpacked[pl.ds(2 * c + 1, windows, stride=2 * share), :]
            weight = scales[:, c : c + 1]
            out_real = weight * (real * cosine + imag * sine)
            out_imag = weight * (imag * cosine - real * sine)
            right[c, 0, t] = jnp.concatenate([out_real, out_imag], axis=1).astype(jnp.bfloat16)
            right[c, 1, t] = jnp.concatenate([out_imag, out_real], axis=1).astype(jnp.bfloat16)
            for j in range(windows):
                one_real = jnp.broadcast_to(out_real[j : j + 1, :], (windows, freq_bins))
                one_imag = jnp.broadcast_to(out_imag[j : j + 1, :], (windows, freq_bins))
                w = t * windows + j
                left[w, c, 0] = jnp.concatenate([one_real, -one_real], axis=1).astype(jnp.bfloat16)
                left[w, c, 1] = jnp.concatenate([one_imag, one_imag], axis=1).astype(jnp.bfloat16)
        return carry

    lax.fori_loop(0, n, align_step, 0)

    def pair_block(t, s):
        for j in range(windows):
            w = t * windows + j
            rows = [left[w, c, 0] * right[c, 0, s] + left[w, c, 1] * right[c, 1, s] for c in range(share)]
            lagged = jnp.dot(jnp.concatenate(rows, axis=0), table[...], preferred_element_type=jnp.float32)
            lagged = lagged.reshape(share, windows, LAGS)
            place = band + windows + s * windows - w
            part[w, pl.ds(place, windows), :] = jnp.sum(lagged * lagged, axis=0)

    def h_copy(t):
        return pltpu.make_async_remote_copy(
            src_ref=half_out.at[t],
            dst_ref=half_in.at[t],
            send_sem=h_send.at[t],
            recv_sem=h_recv.at[t],
            device_id={"chan": 1 - core},
            device_id_type=pl.DeviceIdType.MESH,
        )

    def s_copy(t, slot):
        return pltpu.make_async_remote_copy(
            src_ref=sum_out.at[t],
            dst_ref=sum_in.at[slot],
            send_sem=s_send.at[t],
            recv_sem=s_recv.at[slot],
            device_id={"tm": t},
            device_id_type=pl.DeviceIdType.MESH,
        )

    def pass_on(t):
        h_copy(t).wait_recv()
        return part[pl.ds(t * windows + core * mine, mine), pl.ds(windows, band), :] + half_in[t].astype(jnp.float32)

    def stage(i, carry):
        t = lax.rem(me + 1 + i, n)

        def one_block(s, held):
            pair_block(t, s)
            return held

        lax.fori_loop(jnp.maximum(t - SPAN, 0), t + 1, one_block, 0)
        half_out[t] = part[pl.ds(t * windows + (1 - core) * mine, mine), pl.ds(windows, band), :].astype(jnp.bfloat16)
        h_copy(t).start()

        @pl.when(i > 0)
        def _():
            before = lax.rem(me + i, n)
            sum_out[before] = pass_on(before).astype(jnp.bfloat16)
            s_copy(before, me).start()

        return carry

    lax.fori_loop(0, n, stage, 0)
    result = pass_on(me)
    for d in range(1, n):
        s = lax.rem(me + n - d, n)
        s_copy(s, s).wait_recv()
        result = result + sum_in[s].astype(jnp.float32)
    out_ref[...] = result * (1.0 / (chans * cores))

    for d in range(1, n):
        t = lax.rem(me + d, n)
        x_copy(t, me).wait_send()
        s_copy(t, me).wait_send()
    for t in range(n):
        h_copy(t).wait_send()
    for there, other in others():
        e_copy(there, other, me * cores + core).wait_send()


def spread_shards(spectra, offsets, channel_group):
    windows, chans, _, freq_bins = spectra.shape
    n = lax.axis_size("tm")
    cores = lax.axis_size("chan")
    share = chans // n
    total = n * windows
    band = SPAN * windows
    mine = windows // cores
    dma = pltpu.SemaphoreType.DMA
    return pl.pallas_call(
        functools.partial(kernel, n, chans, windows, share, freq_bins, cores),
        out_shape=jax.ShapeDtypeStruct((mine, band, LAGS), jnp.float32),
        in_specs=[
            pl.BlockSpec(memory_space=pl.ANY),
            pl.BlockSpec(memory_space=pltpu.SMEM),
            pl.BlockSpec(memory_space=pltpu.VMEM),
        ],
        out_specs=pl.BlockSpec(memory_space=pltpu.VMEM),
        scratch_shapes=[
            pltpu.VMEM((windows, 2 * chans, freq_bins), jnp.bfloat16),
            pltpu.VMEM((windows * 2 * chans, freq_bins), jnp.float32),
            pltpu.VMEM((n, windows, 2 * share, freq_bins), jnp.bfloat16),
            pltpu.VMEM((windows * 2 * share, freq_bins), jnp.float32),
            pltpu.VMEM((windows, freq_bins), jnp.float32),
            pltpu.VMEM((n * cores, windows, freq_bins), jnp.float32),
            pltpu.VMEM((2 * freq_bins, LAGS), jnp.bfloat16),
            pltpu.VMEM((share, 2, n, windows, 2 * freq_bins), jnp.bfloat16),
            pltpu.VMEM((total, share, 2, windows, 2 * freq_bins), jnp.bfloat16),
            pltpu.VMEM((total, band + 2 * windows, LAGS), jnp.float32),
            pltpu.VMEM((n, mine, band, LAGS), jnp.bfloat16),
            pltpu.VMEM((n, mine, band, LAGS), jnp.bfloat16),
            pltpu.VMEM((n, mine, band, LAGS), jnp.bfloat16),
            pltpu.VMEM((n, mine, band, LAGS), jnp.bfloat16),
            dma, dma, dma((n,)), dma((n,)), dma((n * cores,)), dma((n * cores,)),
            dma((n,)), dma((n,)), dma((n,)), dma((n,)),
        ],
        compiler_params=pltpu.CompilerParams(
            collective_id=0, has_side_effects=True, vmem_limit_bytes=56 * 1024 * 1024
        ),
    )(spectra.reshape(windows, 2 * chans, freq_bins), offsets, channel_group.reshape(1, chans))


def shards(spectra, offsets, channel_group):
    windows, chans, _, freq_bins = spectra.shape
    n = lax.axis_size("tm")
    fits = (
        chans == freq_bins == LAGS == 128
        and windows == 8
        and lax.axis_size("chan") == 2
        and chans % n == 0
        and chans // n >= 8
    )
    return (spread_shards if fits else ring_shards)(spectra, offsets, channel_group)


def solution(mesh):
    placed = (P(("arrays", "tm"), "chan", None, None), P(("arrays", "tm")), P(("arrays", "chan")))
    return jax.shard_map(
        shards,
        mesh=mesh,
        in_specs=placed,
        out_specs=P(("arrays", "tm", "chan"), None, None),
        check_vma=False,
    )
```

```python
import functools
import math

import jax
import jax.numpy as jnp
from jax import lax
from jax.experimental import pallas as pl
from jax.experimental.pallas import tpu as pltpu
from jax.sharding import PartitionSpec as P

LAGS = 128
GROUPS = 8
SPAN = 6


epsilon = 1e-05


def shifted(value, axis, steps):
    count = lax.axis_size(axis)
    initial, last = (max(0, -steps), min(count, count - steps))
    return lax.ppermute(value, axis, [(source, source + steps) for source in range(initial, last)])


def lag_table(freq_bins, lag_count):
    frequency = jnp.arange(freq_bins, dtype=jnp.int32)[:, None]
    lag_shift = jnp.arange(lag_count, dtype=jnp.int32)[None, :] - lag_count // 2
    phase_turns = jnp.mod(frequency * lag_shift, 2 * freq_bins).astype(jnp.float32)
    phase_angle = jnp.pi * phase_turns / freq_bins
    normaliser = 1.0 / math.sqrt(freq_bins)
    lag_rows = jnp.concatenate(
        [jnp.cos(phase_angle) * normaliser, -jnp.sin(phase_angle) * normaliser], axis=0
    )
    return lag_rows.astype(jnp.bfloat16)


def align_spectra(spectra, offsets, scales):
    freq_bins = spectra.shape[3]
    frequency = jnp.arange(freq_bins, dtype=jnp.int32)[None, :]
    phase_turns = jnp.mod(offsets[:, None] * frequency, 2 * freq_bins).astype(jnp.float32)
    phase_angle = jnp.pi * phase_turns / freq_bins
    cosine = jnp.cos(phase_angle)[:, None, :]
    sine_part = jnp.sin(phase_angle)[:, None, :]
    real_part = spectra[:, :, 0, :].astype(jnp.float32)
    imag_part = spectra[:, :, 1, :].astype(jnp.float32)
    weight = scales[:, :, None]
    out_real = weight * (real_part * cosine + imag_part * sine_part)
    out_imag = weight * (imag_part * cosine - real_part * sine_part)
    return jnp.stack([out_real, out_imag], axis=2).astype(jnp.bfloat16)


def window_terms(current, band_rows, lag_rows):
    left_real = current[None, :, 0, :].astype(jnp.float32)
    left_imag = current[None, :, 1, :].astype(jnp.float32)
    right_real = band_rows[:, :, 0, :].astype(jnp.float32)
    right_imag = band_rows[:, :, 1, :].astype(jnp.float32)
    prod_real = left_real * right_real + left_imag * right_imag
    prod_imag = left_imag * right_real - left_real * right_imag
    cross_spec = jnp.stack([prod_real, prod_imag], axis=2).astype(jnp.bfloat16)
    flattened = cross_spec.reshape(band_rows.shape[0] * band_rows.shape[1], 2 * band_rows.shape[3])
    lagged = jnp.dot(flattened, lag_rows, preferred_element_type=jnp.float32)
    lagged = lagged.reshape(band_rows.shape[0], band_rows.shape[1], lag_rows.shape[1])
    return jnp.sum(lagged * lagged, axis=1)


def ring_shards(spectra, offsets, channel_group):
    windows = spectra.shape[0]
    local_chans = spectra.shape[1]
    freq_bins = spectra.shape[3]
    chan_count = lax.axis_size("chan")
    channels = local_chans * chan_count
    onehot = (channel_group[:, None] == jnp.arange(GROUPS, dtype=jnp.int32)[None, :]).astype(
        jnp.float32
    )
    chan_power = jnp.sum(jnp.square(spectra.astype(jnp.float32)), axis=(2, 3))
    partial_value = jnp.dot(chan_power, onehot, precision=lax.Precision.HIGHEST)
    group_total = lax.psum(partial_value, "chan")
    energy = group_total * (GROUPS / (freq_bins * channels))
    scales = jnp.dot(lax.rsqrt(energy + epsilon), onehot.T, precision=lax.Precision.HIGHEST)
    aligned = align_spectra(spectra, offsets, scales)
    earlier = []
    carried = aligned
    for distance in range(SPAN):
        carried = shifted(carried, "tm", 1)
        earlier.append(carried)
    buffer = jnp.concatenate(earlier[::-1] + [aligned], axis=0)
    lag_rows = lag_table(freq_bins, LAGS)
    band_len = SPAN * windows

    def one_window(window):
        current = lax.dynamic_index_in_dim(aligned, window, 0, keepdims=False)
        band_rows = lax.dynamic_slice_in_dim(buffer, window, band_len, 0)
        return window_terms(current, band_rows, lag_rows) * (1.0 / channels)

    return lax.psum_scatter(
        lax.map(
            one_window, jnp.arange(lax.axis_size("chan") * (windows // chan_count), dtype=jnp.int32)
        ).astype(jnp.bfloat16),
        "chan",
        scatter_dimension=0,
        tiled=True,
    ).astype(jnp.float32)


LATE = 4
HIGHEST = lax.Precision.HIGHEST


def phase_of(turns, freq_bins):
    period = 2.0 * freq_bins
    return (jnp.pi / freq_bins) * (turns - period * jnp.floor(turns / period))


def kernel(
    n, chans, windows, share, freq_bins, cores,
    x_ref, off_ref, group_ref, out_ref,
    local, wide, raw, unpacked, tile, tiles, table, right, left, part, half_out, half_in, sum_out, sum_in,
    local_sem, keep_sem, x_send, x_recv, e_send, e_recv, h_send, h_recv, s_send, s_recv,
):
    me = lax.axis_index("tm")
    core = lax.axis_index("chan")
    band = SPAN * windows
    mine = windows // cores
    lanes = freq_bins

    load = pltpu.make_async_copy(x_ref, local, local_sem)
    load.start()
    keep = pltpu.make_async_copy(x_ref.at[:, pl.ds(me * 2 * share, 2 * share), :], raw.at[me], keep_sem)
    keep.start()

    barrier = pltpu.get_barrier_semaphore()
    for d in range(n):
        for k in range(cores):
            if d or k:
                pl.semaphore_signal(
                    barrier, inc=1,
                    device_id={"tm": lax.rem(me + d, n), "chan": lax.rem(core + k, cores)},
                    device_id_type=pl.DeviceIdType.MESH,
                )
    def x_copy(there, slot):
        return pltpu.make_async_remote_copy(
            src_ref=x_ref.at[:, pl.ds(there * 2 * share, 2 * share), :],
            dst_ref=raw.at[slot],
            send_sem=x_send.at[there],
            recv_sem=x_recv.at[slot],
            device_id={"tm": there},
            device_id_type=pl.DeviceIdType.MESH,
        )

    load.wait()
    for w in range(windows):
        wide[pl.ds(w * 2 * chans, 2 * chans), :] = local[w].astype(jnp.float32)
    lane = lax.broadcasted_iota(jnp.int32, (windows, lanes), 1)
    row = lax.broadcasted_iota(jnp.int32, (windows, lanes), 0)

    def power_step(c, held):
        real = wide[pl.ds(2 * c, windows, stride=2 * chans), :]
        imag = wide[pl.ds(2 * c + 1, windows, stride=2 * chans), :]
        power = jnp.sum(real * real + imag * imag, axis=1, keepdims=True)
        return jnp.where(lane == c, power, held)

    chan_power = lax.fori_loop(0, chans, power_step, jnp.zeros((windows, lanes), jnp.float32), unroll=8)
    group_id = lax.broadcasted_iota(jnp.int32, (lanes, chans), 0)
    onehot = (group_id == group_ref[...]).astype(jnp.float32)
    totals = lax.dot_general(
        chan_power, onehot, (((1,), (1,)), ((), ())), precision=HIGHEST, preferred_element_type=jnp.float32
    )
    for w in range(windows):
        totals = jnp.where((lane == lanes - 1) & (row == w), off_ref[w].astype(jnp.float32), totals)
    tile[...] = totals

    def e_copy(there, other, slot):
        return pltpu.make_async_remote_copy(
            src_ref=tile,
            dst_ref=tiles.at[slot],
            send_sem=e_send.at[there * cores + other],
            recv_sem=e_recv.at[slot],
            device_id={"tm": there, "chan": other},
            device_id_type=pl.DeviceIdType.MESH,
        )

    def others():
        for d in range(n):
            for k in range(cores):
                if d or k:
                    yield lax.rem(me + d, n), lax.rem(core + k, cores)

    pl.semaphore_wait(barrier, n * cores - 1)
    for there, other in others():
        e_copy(there, other, me * cores + core).start()
    for d in range(1, n):
        x_copy(lax.rem(me + d, n), me).start()
    tiles[me * cores + core] = totals

    frequency = lax.broadcasted_iota(jnp.int32, (freq_bins, LAGS), 0)
    shift = lax.broadcasted_iota(jnp.int32, (freq_bins, LAGS), 1) - LAGS // 2
    angle = phase_of((frequency * shift).astype(jnp.float32), freq_bins)
    normaliser = 1.0 / math.sqrt(freq_bins)
    table[pl.ds(0, freq_bins), :] = (jnp.cos(angle) * normaliser).astype(jnp.bfloat16)
    table[pl.ds(freq_bins, freq_bins), :] = (-jnp.sin(angle) * normaliser).astype(jnp.bfloat16)
    part[...] = jnp.zeros_like(part)

    my_onehot = (group_id == pltpu.roll(group_ref[...], lax.rem(chans - me * share, chans), 1)).astype(jnp.float32)
    bins = lax.broadcasted_iota(jnp.int32, (windows, freq_bins), 1).astype(jnp.float32)
    keep.wait()
    for there, other in others():
        e_copy(there, other, there * cores + other).wait_recv()

    early = n - LATE

    def pair_block(t, s):
        for j in range(windows):
            w = t * windows + j
            rows = [left[w, c, 0] * right[c, 0, s] + left[w, c, 1] * right[c, 1, s] for c in range(share)]
            lagged = jnp.dot(jnp.concatenate(rows, axis=0), table[...], preferred_element_type=jnp.float32)
            lagged = lagged.reshape(share, windows, LAGS)
            place = band + windows + s * windows - w
            part[w, pl.ds(place, windows), :] = jnp.sum(lagged * lagged, axis=0)

    def align_step(i, carry):
        t = lax.rem(me + n - i, n)

        @pl.when(i > 0)
        def _():
            x_copy(t, t).wait_recv()

        for w in range(windows):
            unpacked[pl.ds(w * 2 * share, 2 * share), :] = raw[t, w].astype(jnp.float32)
        first = tiles[t * cores]
        summed = first
        for k in range(1, cores):
            summed = summed + tiles[t * cores + k]
        energy = summed * (GROUPS / (freq_bins * chans * cores))
        scales = jnp.dot(
            lax.rsqrt(energy + epsilon), my_onehot, precision=HIGHEST, preferred_element_type=jnp.float32
        )
        theta = phase_of(bins * first[:, lanes - 1 : lanes], freq_bins)
        cosine = jnp.cos(theta)
        sine = jnp.sin(theta)
        for c in range(share):
            real = unpacked[pl.ds(2 * c, windows, stride=2 * share), :]
            imag = unpacked[pl.ds(2 * c + 1, windows, stride=2 * share), :]
            weight = scales[:, c : c + 1]
            out_real = weight * (real * cosine + imag * sine)
            out_imag = weight * (imag * cosine - real * sine)
            right[c, 0, t] = jnp.concatenate([out_real, out_imag], axis=1).astype(jnp.bfloat16)
            right[c, 1, t] = jnp.concatenate([out_imag, out_real], axis=1).astype(jnp.bfloat16)
            for j in range(windows):
                one_real = jnp.broadcast_to(out_real[j : j + 1, :], (windows, freq_bins))
                one_imag = jnp.broadcast_to(out_imag[j : j + 1, :], (windows, freq_bins))
                w = t * windows + j
                left[w, c, 0] = jnp.concatenate([one_real, -one_real], axis=1).astype(jnp.bfloat16)
                left[w, c, 1] = jnp.concatenate([one_imag, one_imag], axis=1).astype(jnp.bfloat16)

        def known_pair(k, held):
            other = lax.rem(me + n - k, n)
            upper, lower = jnp.maximum(t, other), jnp.minimum(t, other)

            @pl.when(upper - lower <= SPAN)
            def _():
                pair_block(upper, lower)

            return held

        @pl.when(i < early)
        def _():
            lax.fori_loop(0, i + 1, known_pair, 0)

        return carry

    lax.fori_loop(0, n, align_step, 0)

    def h_copy(t):
        return pltpu.make_async_remote_copy(
            src_ref=half_out.at[t],
            dst_ref=half_in.at[t],
            send_sem=h_send.at[t],
            recv_sem=h_recv.at[t],
            device_id={"chan": 1 - core},
            device_id_type=pl.DeviceIdType.MESH,
        )

    def s_copy(t, slot):
        return pltpu.make_async_remote_copy(
            src_ref=sum_out.at[t],
            dst_ref=sum_in.at[slot],
            send_sem=s_send.at[t],
            recv_sem=s_recv.at[slot],
            device_id={"tm": t},
            device_id_type=pl.DeviceIdType.MESH,
        )

    def pass_on(t):
        h_copy(t).wait_recv()
        return part[pl.ds(t * windows + core * mine, mine), pl.ds(windows, band), :] + half_in[t].astype(jnp.float32)

    def stage(i, carry):
        t = lax.rem(me + 1 + i, n)

        def one_block(s, held):
            behind = jnp.maximum(lax.rem(me - t + n, n), lax.rem(me - s + n, n))

            @pl.when(behind >= early)
            def _():
                pair_block(t, s)

            return held

        lax.fori_loop(jnp.maximum(t - SPAN, 0), t + 1, one_block, 0)
        half_out[t] = part[pl.ds(t * windows + (1 - core) * mine, mine), pl.ds(windows, band), :].astype(jnp.bfloat16)
        h_copy(t).start()

        @pl.when(i > 0)
        def _():
            before = lax.rem(me + i, n)
            sum_out[before] = pass_on(before).astype(jnp.bfloat16)
            s_copy(before, me).start()

        return carry

    lax.fori_loop(0, n, stage, 0)
    result = pass_on(me)
    for d in range(1, n):
        s = lax.rem(me + n - d, n)
        s_copy(s, s).wait_recv()
        result = result + sum_in[s].astype(jnp.float32)
    out_ref[...] = result * (1.0 / (chans * cores))

    for d in range(1, n):
        t = lax.rem(me + d, n)
        x_copy(t, me).wait_send()
        s_copy(t, me).wait_send()
    for t in range(n):
        h_copy(t).wait_send()
    for there, other in others():
        e_copy(there, other, me * cores + core).wait_send()


def spread_shards(spectra, offsets, channel_group):
    windows, chans, _, freq_bins = spectra.shape
    n = lax.axis_size("tm")
    cores = lax.axis_size("chan")
    share = chans // n
    total = n * windows
    band = SPAN * windows
    mine = windows // cores
    dma = pltpu.SemaphoreType.DMA
    return pl.pallas_call(
        functools.partial(kernel, n, chans, windows, share, freq_bins, cores),
        out_shape=jax.ShapeDtypeStruct((mine, band, LAGS), jnp.float32),
        in_specs=[
            pl.BlockSpec(memory_space=pl.ANY),
            pl.BlockSpec(memory_space=pltpu.SMEM),
            pl.BlockSpec(memory_space=pltpu.VMEM),
        ],
        out_specs=pl.BlockSpec(memory_space=pltpu.VMEM),
        scratch_shapes=[
            pltpu.VMEM((windows, 2 * chans, freq_bins), jnp.bfloat16),
            pltpu.VMEM((windows * 2 * chans, freq_bins), jnp.float32),
            pltpu.VMEM((n, windows, 2 * share, freq_bins), jnp.bfloat16),
            pltpu.VMEM((windows * 2 * share, freq_bins), jnp.float32),
            pltpu.VMEM((windows, freq_bins), jnp.float32),
            pltpu.VMEM((n * cores, windows, freq_bins), jnp.float32),
            pltpu.VMEM((2 * freq_bins, LAGS), jnp.bfloat16),
            pltpu.VMEM((share, 2, n, windows, 2 * freq_bins), jnp.bfloat16),
            pltpu.VMEM((total, share, 2, windows, 2 * freq_bins), jnp.bfloat16),
            pltpu.VMEM((total, band + 2 * windows, LAGS), jnp.float32),
            pltpu.VMEM((n, mine, band, LAGS), jnp.bfloat16),
            pltpu.VMEM((n, mine, band, LAGS), jnp.bfloat16),
            pltpu.VMEM((n, mine, band, LAGS), jnp.bfloat16),
            pltpu.VMEM((n, mine, band, LAGS), jnp.bfloat16),
            dma, dma, dma((n,)), dma((n,)), dma((n * cores,)), dma((n * cores,)),
            dma((n,)), dma((n,)), dma((n,)), dma((n,)),
        ],
        compiler_params=pltpu.CompilerParams(
            collective_id=0, has_side_effects=True, vmem_limit_bytes=56 * 1024 * 1024
        ),
    )(spectra.reshape(windows, 2 * chans, freq_bins), offsets, channel_group.reshape(1, chans))


def shards(spectra, offsets, channel_group):
    windows, chans, _, freq_bins = spectra.shape
    n = lax.axis_size("tm")
    fits = (
        chans == freq_bins == LAGS == 128
        and windows == 8
        and lax.axis_size("chan") == 2
        and chans % n == 0
        and chans // n >= 8
    )
    return (spread_shards if fits else ring_shards)(spectra, offsets, channel_group)


def solution(mesh):
    placed = (P(("arrays", "tm"), "chan", None, None), P(("arrays", "tm")), P(("arrays", "chan")))
    return jax.shard_map(
        shards,
        mesh=mesh,
        in_specs=placed,
        out_specs=P(("arrays", "tm", "chan"), None, None),
        check_vma=False,
    )
```
